256 devices in a mesh: gx: 8 (over z_hi, y), gz: 32 (over x, z_lo, core).
Axes of the slice: x: 4, y: 4, z: 8 (z_hi: 2, z_lo: 4; z = z_hi * 4 + z_lo), core: 2. Of those that a mesh axis runs over, the one named last changes fastest.
Arguments:
- state: float32 [5, 16, 128, 512], P(None, 'gx', 'gz'), may hold values from -21 to 21
- cotangent: float32 [5, 16, 128, 512], P(None, 'gx', 'gz'), may hold values from -6 to 6
- local_inverse: float32 [64, 16, 128, 512], P(None, 'gx', 'gz'), may hold values from -0.25 to 1.7
- wall_tags: int32 [2, 16, 128], P(None, 'gx', 'gz'), may hold values 0 or 1
- w_in: float32 [5, 256], replicated, may hold values from -2.5 to 2.5
- b_in: float32 [256], replicated, may hold values from -3 to 3
- w_mid: bfloat16 [256, 256], replicated, may hold values from -0.375 to 0.375
- b_mid: float32 [256], replicated, may hold values from -3 to 3
- w_out: bfloat16 [256, 5], replicated, may hold values from -1.5 to 1.5
Outputs:
- grad_state: float32 [5, 16, 128, 512], P(None, 'gx', 'gz')
- grad_w_in: float32 [5, 256], replicated
- grad_b_in: float32 [256], replicated
- grad_w_mid: float32 [256, 256], replicated
- grad_b_mid: float32 [256], replicated
- grad_w_out: float32 [256, 5], replicated
The draws below stay inside these ranges and needn't reach their ends.
All inputs are finite; a program needn't handle non-finite values. No bound on the sum of `wall_tags` on one device may be relied on, other than what follows from the above.
Results may differ from the reference program's by a relative error of at most 0.0085.
Values sent between devices are 32-bit elements; how exact they have to be, the bound alone decides.
No kernel may reach another device: no remote copies, remote signals or barrier semaphores. Data moves between devices by JAX's collectives and lax.ppermute only.
A program may use at most 64 MiB of HBM per device.

```python
import math
import jax
import jax.numpy as jnp
from jax import lax

C = 5
H = 256
P_SIZE = 64
EY = 8
NXE = 16
NZE = 128


def draw_state(key, part):
    first_key, second_key = jax.random.split(key)
    x_pos = jnp.arange(NXE, dtype=jnp.float32) / max(NXE - 1, 1)
    z_pos = jnp.arange(NZE, dtype=jnp.float32) / max(NZE - 1, 1)
    ramp = (1.0 + 2.0 * x_pos)[:, None, None] * (1.0 + 2.0 * z_pos)[None, :, None]
    rough = jax.random.uniform(second_key, (NXE, NZE, EY), jnp.float32, 0.5, 1.5)
    amplitude = jnp.repeat(ramp * rough, P_SIZE, axis=2)
    values = jax.random.truncated_normal(first_key, -3.0, 3.0, (C, NXE, NZE, EY * P_SIZE), jnp.float32)
    return 0.5 * amplitude[None] * values


def draw_local_inverse(key, part):
    first_key, second_key = jax.random.split(key)
    diagonal = jax.random.uniform(first_key, (NXE, NZE, EY, P_SIZE), jnp.float32, 0.6, 1.4)
    spread = 0.075 * jax.random.truncated_normal(second_key, -3.0, 3.0, (P_SIZE, NXE, NZE, EY * P_SIZE), jnp.float32)
    identity = jnp.eye(P_SIZE, dtype=jnp.float32)[:, None, None, None, :]
    diag_part = (identity * diagonal[None]).reshape(P_SIZE, NXE, NZE, EY * P_SIZE)
    return spread + diag_part


def set_ends(drawn, key, smallest, top_value):
    spot = [jax.random.randint(jax.random.fold_in(key, axis), (), 0, length) for axis, length in enumerate(drawn.shape)]
    main_axis = drawn.shape.index(max(drawn.shape))
    beside = spot[:main_axis] + [(spot[main_axis] + 1) % drawn.shape[main_axis]] + spot[main_axis + 1:]
    return drawn.at[tuple(spot)].set(smallest).at[tuple(beside)].set(top_value)


def shard_levels(own_key, shape, pieces, least, largest):
    factor_of, own = 1.0, jax.random.fold_in(own_key, 6)
    for position, shards_of in pieces:
        steps = jnp.exp(jax.random.uniform(jax.random.fold_in(own, position), (shards_of,), jnp.float32, least / len(pieces), largest / len(pieces)))
        factor_of = factor_of * jnp.repeat(steps, shape[position] // shards_of).reshape([-1 if axis == position else 1 for axis in range(len(shape))])
    return factor_of


def normal_values(stream_key, extent, deviation, most, cuts=(), held_as=jnp.bfloat16):
    values = deviation * jax.random.normal(stream_key, extent, jnp.float32)
    if cuts:
        values = values * shard_levels(stream_key, extent, cuts, -0.22, 0.18)
    return jnp.clip(values, -most, most).astype(held_as)


def setup_inputs(seed: int = 0) -> dict:
    streams_of = jax.random.split(jax.random.key(seed), 10)
    return {
        "state": draw_state(jax.random.fold_in(streams_of[9], 71), 0),
        "cotangent": normal_values(streams_of[1], (C, NXE, NZE, EY * P_SIZE), 1.0, 6.0, ((1, 8), (2, 32)), jnp.float32),
        "local_inverse": draw_local_inverse(jax.random.fold_in(streams_of[9], 71), 0),
        "wall_tags": set_ends((jax.random.randint(streams_of[3], (2, NXE, NZE), 0, 2) < 1).astype(jnp.int32), jax.random.fold_in(streams_of[3], 1), 0, 1),
        "w_in": normal_values(streams_of[4], (C, H), C ** -0.5, 2.5, (), jnp.float32),
        "b_in": normal_values(streams_of[5], (H,), 0.5, 3.0, (), jnp.float32),
        "w_mid": normal_values(streams_of[6], (H, H), H ** -0.5, 0.375),
        "b_mid": normal_values(streams_of[7], (H,), 0.5, 3.0, (), jnp.float32),
        "w_out": normal_values(streams_of[8], (H, C), (H // 16) ** -0.5, 1.5),
    }


KAPPA = 0.5
DT_STEP = 0.5
EPS = 1e-06
precise = lax.Precision.HIGHEST

def silu_slope(pre_act):
    sigmoid_value = jax.nn.sigmoid(pre_act)
    return sigmoid_value * (1.0 + pre_act * (1.0 - sigmoid_value))

def inner_rows(first_op, second_op, precision=None):
    return lax.dot_general(first_op, second_op, (((1,), (1,)), ((), ())), precision=precision, preferred_element_type=jnp.float32)

def inner_first(first_op, second_op, precision=None):
    return lax.dot_general(first_op, second_op, (((0,), (0,)), ((), ())), precision=precision, preferred_element_type=jnp.float32)

def face_terms(blocks_view, lower_nb, upper_nb, face_axis):
    lower_term = 0.5 * (lower_nb - jnp.take(blocks_view, 0, axis=face_axis))
    upper_term = 0.5 * (upper_nb - jnp.take(blocks_view, 3, axis=face_axis))
    zero_face = jnp.zeros_like(lower_term)
    return jnp.stack([lower_term, zero_face, zero_face, upper_term], axis=face_axis)

def coupling(blocks_view, lower_x, upper_x, lower_z, upper_z, wall_tags):
    bottom = (1.0 - 2.0 * wall_tags[0].astype(jnp.float32))[None, :, :, None, None, None]
    top_side = (1.0 - 2.0 * wall_tags[1].astype(jnp.float32))[None, :, :, None, None, None]
    lower_y = jnp.concatenate([bottom * blocks_view[:, :, :, :1, :, 0, :], blocks_view[:, :, :, :-1, :, 3, :]], axis=3)
    upper_y = jnp.concatenate([blocks_view[:, :, :, 1:, :, 0, :], top_side * blocks_view[:, :, :, -1:, :, 3, :]], axis=3)
    return face_terms(blocks_view, lower_x, upper_x, 4) + face_terms(blocks_view, lower_y, upper_y, 5) + face_terms(blocks_view, lower_z, upper_z, 6)

def reference(state, cotangent, local_inverse, wall_tags, w_in, b_in, w_mid, b_mid, w_out):
    line_nodes = EY * P_SIZE
    entry_count = C * NXE * NZE * line_nodes
    inv_norm = lax.rsqrt(jnp.sum(state * state) / entry_count + EPS)
    adjoint = jnp.einsum('nikjm,cikjn->cikjm', local_inverse.reshape(P_SIZE, NXE, NZE, EY, P_SIZE), cotangent.reshape(C, NXE, NZE, EY, P_SIZE), precision=precise)
    blocks_view = adjoint.reshape(C, NXE, NZE, EY, 4, 4, 4)
    lower_x = jnp.roll(blocks_view[:, :, :, :, 3], 1, axis=1)
    upper_x = jnp.roll(blocks_view[:, :, :, :, 0], -1, axis=1)
    lower_z = jnp.roll(blocks_view[..., 3], 1, axis=2)
    upper_z = jnp.roll(blocks_view[..., 0], -1, axis=2)
    coupled = coupling(blocks_view, lower_x, upper_x, lower_z, upper_z, wall_tags).reshape(C, NXE, NZE, line_nodes)
    adjoint_flat = adjoint.reshape(C, NXE, NZE, line_nodes)

    def column(carry, inputs):
        state_block, adjoint_block = inputs
        state_rows = state_block.reshape(C, NZE * line_nodes)
        adjoint_rows = adjoint_block.reshape(C, NZE * line_nodes)
        scaled_rows = inv_norm * state_rows
        pre_first = inner_first(w_in, scaled_rows, precise) + b_in[:, None]
        hidden_one = jax.nn.silu(pre_first).astype(jnp.bfloat16)
        pre_second = inner_first(w_mid, hidden_one) + b_mid[:, None]
        hidden_two = jax.nn.silu(pre_second).astype(jnp.bfloat16)
        out_grad = (DT_STEP * adjoint_rows).astype(jnp.bfloat16)
        grad_out = inner_rows(hidden_two, out_grad)
        back_two = jnp.dot(w_out, out_grad, preferred_element_type=jnp.float32)
        delta_two = (back_two * silu_slope(pre_second)).astype(jnp.bfloat16)
        grad_mid = inner_rows(hidden_one, delta_two)
        grad_bmid = lax.optimization_barrier(jnp.sum(delta_two.astype(jnp.float32), axis=1))
        back_one = jnp.dot(w_mid, delta_two, preferred_element_type=jnp.float32)
        delta_one = back_one * silu_slope(pre_first)
        grad_in = inner_rows(scaled_rows, delta_one, precise)
        grad_bin = lax.optimization_barrier(jnp.sum(delta_one, axis=1))
        back_input = jnp.dot(w_in, delta_one, precision=precise, preferred_element_type=jnp.float32)
        new_carry = (carry[0] + grad_in, carry[1] + grad_bin, carry[2] + grad_mid, carry[3] + grad_bmid, carry[4] + grad_out)
        return (new_carry, back_input)
    start = (jnp.zeros((C, H), jnp.float32), jnp.zeros((H,), jnp.float32), jnp.zeros((H, H), jnp.float32), jnp.zeros((H,), jnp.float32), jnp.zeros((H, C), jnp.float32))
    totals, back_blocks = lax.scan(column, start, (jnp.moveaxis(state, 1, 0), jnp.moveaxis(adjoint_flat, 1, 0)))
    back_input = jnp.moveaxis(back_blocks.reshape(NXE, C, NZE, line_nodes), 0, 1)
    grad_state = adjoint_flat + KAPPA * coupled + inv_norm * back_input
    factor = 4.0 / math.sqrt(NXE * NZE * line_nodes)
    return (grad_state, totals[0] * factor, totals[1] * factor, totals[2] * factor, totals[3] * factor, totals[4] * factor)
```

```python
import math

import jax
import jax.numpy as jnp
import numpy as np
from jax import lax
from jax.sharding import Mesh, PartitionSpec as P

KAPPA = 0.5
DT_STEP = 0.5
EPS = 1e-06
precise = lax.Precision.HIGHEST

AXES = ("zhi", "y", "x", "zlo", "core")
GX = ("zhi", "y")
GZ = ("x", "zlo", "core")
CHIPS = ("zhi", "y", "x", "zlo")


def silu_slope(pre_act):
    sigmoid_value = jax.nn.sigmoid(pre_act)
    return sigmoid_value * (1.0 + pre_act * (1.0 - sigmoid_value))


def inner_rows(first_op, second_op, precision=None):
    return lax.dot_general(
        first_op,
        second_op,
        (((1,), (1,)), ((), ())),
        precision=precision,
        preferred_element_type=jnp.float32,
    )


def inner_first(first_op, second_op, precision=None):
    return lax.dot_general(
        first_op,
        second_op,
        (((0,), (0,)), ((), ())),
        precision=precision,
        preferred_element_type=jnp.float32,
    )


def face_terms(blocks_view, lower_nb, upper_nb, face_axis):
    lower_term = 0.5 * (lower_nb - jnp.take(blocks_view, 0, axis=face_axis))
    upper_term = 0.5 * (upper_nb - jnp.take(blocks_view, 3, axis=face_axis))
    zero_face = jnp.zeros_like(lower_term)
    return jnp.stack([lower_term, zero_face, zero_face, upper_term], axis=face_axis)


def coupling(blocks_view, lower_x, upper_x, lower_z, upper_z, wall_tags):
    bottom = (1.0 - 2.0 * wall_tags[0].astype(jnp.float32))[None, :, :, None, None, None]
    top_side = (1.0 - 2.0 * wall_tags[1].astype(jnp.float32))[None, :, :, None, None, None]
    lower_y = jnp.concatenate(
        [bottom * blocks_view[:, :, :, :1, :, 0, :], blocks_view[:, :, :, :-1, :, 3, :]], axis=3
    )
    upper_y = jnp.concatenate(
        [blocks_view[:, :, :, 1:, :, 0, :], top_side * blocks_view[:, :, :, -1:, :, 3, :]], axis=3
    )
    return (
        face_terms(blocks_view, lower_x, upper_x, 4)
        + face_terms(blocks_view, lower_y, upper_y, 5)
        + face_terms(blocks_view, lower_z, upper_z, 6)
    )


def ring(count, step):
    return [(i, (i + step) % count) for i in range(count)]


def all_devices_sum(value, count):
    spread = jnp.broadcast_to(value, (count, 1, 128))
    return jnp.sum(lax.all_to_all(spread, AXES, 0, 0, tiled=True)[:, 0, 0])


def reduce_everywhere(packed, chips, factor):
    rows, width = packed.shape
    halves = packed.reshape(2, rows // 2, width)
    core = lax.axis_index("core")
    swap = [(0, 1), (1, 0)]
    mine = lax.dynamic_index_in_dim(halves, core, 0, False)
    other = lax.dynamic_index_in_dim(halves, 1 - core, 0, False)
    mine = mine + lax.ppermute(other, "core", swap)
    scattered = lax.all_to_all(mine.reshape(chips, -1, width), CHIPS, 0, 0, tiled=True)
    chunk = factor * jnp.sum(scattered, axis=0)
    chunk = lax.optimization_barrier(chunk)
    gathered = lax.all_to_all(
        jnp.broadcast_to(chunk[None], (chips,) + chunk.shape), CHIPS, 0, 0, tiled=True
    )
    gathered = lax.optimization_barrier(gathered)
    partner = lax.ppermute(gathered, "core", swap)
    first = jnp.where(core == 0, gathered, partner)
    second = jnp.where(core == 0, partner, gathered)
    return jnp.concatenate([first, second], axis=0).reshape(rows, width)


def per_device(state, cotangent, local_inverse, wall_tags, w_in, b_in, w_mid, b_mid, w_out):
    channels, x_elems, z_elems, line_nodes = state.shape
    y_elems = line_nodes // 64
    node_rows = x_elems * z_elems * line_nodes
    gx, gz = lax.axis_size(GX), lax.axis_size(GZ)
    entry_count = channels * node_rows * gx * gz
    sum_squares = all_devices_sum(jnp.sum(state * state), gx * gz)
    inv_norm = lax.rsqrt(sum_squares / entry_count + EPS)
    adjoint = jnp.einsum(
        "nikjm,cikjn->cikjm",
        local_inverse.reshape(64, x_elems, z_elems, y_elems, 64),
        cotangent.reshape(channels, x_elems, z_elems, y_elems, 64),
        precision=precise,
    )
    adjoint_flat = adjoint.reshape(channels, x_elems, z_elems, line_nodes)
    blocks_view = adjoint.reshape(channels, x_elems, z_elems, y_elems, 4, 4, 4)
    from_left = lax.ppermute(blocks_view[:, -1:, :, :, 3], GX, ring(gx, 1))
    from_right = lax.ppermute(blocks_view[:, :1, :, :, 0], GX, ring(gx, -1))
    from_front = lax.ppermute(blocks_view[:, :, -1:, :, :, :, 3], GZ, ring(gz, 1))
    from_back = lax.ppermute(blocks_view[:, :, :1, :, :, :, 0], GZ, ring(gz, -1))
    lower_x = jnp.concatenate([from_left, blocks_view[:, :-1, :, :, 3]], axis=1)
    upper_x = jnp.concatenate([blocks_view[:, 1:, :, :, 0], from_right], axis=1)
    lower_z = jnp.concatenate([from_front, blocks_view[:, :, :-1, :, :, :, 3]], axis=2)
    upper_z = jnp.concatenate([blocks_view[:, :, 1:, :, :, :, 0], from_back], axis=2)
    coupled = coupling(blocks_view, lower_x, upper_x, lower_z, upper_z, wall_tags).reshape(
        channels, x_elems, z_elems, line_nodes
    )
    state_rows = state.reshape(channels, node_rows)
    scaled_rows = inv_norm * state_rows
    pre_first = inner_first(w_in, scaled_rows, precise) + b_in[:, None]
    hidden_one = jax.nn.silu(pre_first).astype(jnp.bfloat16)
    pre_second = inner_first(w_mid, hidden_one) + b_mid[:, None]
    hidden_two = jax.nn.silu(pre_second).astype(jnp.bfloat16)
    out_grad = (DT_STEP * adjoint_flat.reshape(channels, node_rows)).astype(jnp.bfloat16)
    grad_out = inner_rows(hidden_two, out_grad)
    back_two = jnp.dot(w_out, out_grad, preferred_element_type=jnp.float32)
    delta_two = (back_two * silu_slope(pre_second)).astype(jnp.bfloat16)
    grad_mid = inner_rows(hidden_one, delta_two)
    grad_bmid = jnp.sum(delta_two, axis=1, dtype=jnp.float32)
    back_one = jnp.dot(w_mid, delta_two, preferred_element_type=jnp.float32)
    delta_one = back_one * silu_slope(pre_first)
    grad_in = inner_rows(delta_one, scaled_rows, precise)
    grad_bin = jnp.sum(delta_one, axis=1)
    back_input = jnp.dot(w_in, delta_one, precision=precise, preferred_element_type=jnp.float32)
    grad_state = (
        adjoint_flat
        + KAPPA * coupled
        + inv_norm * back_input.reshape(channels, x_elems, z_elems, line_nodes)
    )
    factor = 4.0 / math.sqrt(entry_count // channels)
    hidden = w_mid.shape[0]
    pad = jnp.zeros((hidden, 384 - hidden - 2 * channels - 2), jnp.float32)
    packed = jnp.concatenate(
        [grad_mid, grad_in, grad_out, grad_bin[:, None], grad_bmid[:, None], pad], axis=1
    )
    summed = reduce_everywhere(packed, gx * gz // 2, factor)
    h, c = hidden, channels
    return (
        grad_state,
        summed[:, h : h + c].T,
        summed[:, h + 2 * c],
        summed[:, :h],
        summed[:, h + 2 * c + 1],
        summed[:, h + c : h + 2 * c],
    )


def solution(mesh):
    fine = Mesh(mesh.devices.reshape(2, 4, 4, 4, 2), AXES)
    block = P(None, GX, GZ, None)
    placed = (block, block, block, P(None, GX, GZ)) + (P(),) * 5
    return jax.shard_map(
        per_device,
        mesh=fine,
        in_specs=placed,
        out_specs=(block, P(), P(), P(), P(), P()),
        check_vma=False,
    )
```

```python
import functools
import math

import jax
import jax.numpy as jnp
from jax import lax
from jax.experimental import pallas as pl
from jax.experimental.pallas import tpu as pltpu
from jax.sharding import Mesh, PartitionSpec as P

KAPPA = 0.5
DT_STEP = 0.5
EPS = 1e-06

AXES = ("zhi", "y", "x", "zlo", "core")
GX = ("zhi", "y")
GZ = ("x", "zlo", "core")
CHIPS = ("zhi", "y", "x", "zlo")
LANES = 128
NODES = 64
GROUP = 8
F32 = jnp.float32
BF16 = jnp.bfloat16


def whole_vmem(count):
    return [pl.BlockSpec(memory_space=pltpu.VMEM)] * count


def rows_of(ref, *lead):
    return jnp.concatenate([ref[lead + (0,)], ref[lead + (1,)]], axis=0)


def adjoint_kernel(
    state_ref, cot_ref, inv_ref, w_mid_ref, b_mid_ref,
    adj_ref, og_ref, xs_ref, w_mid_t_ref, b_col_ref, left_ref, right_ref, front_ref, back_ref,
    rows_ref,
):
    channels, _, span, line = state_ref.shape
    tiles = line // LANES
    cells = 2 * span
    cots = []
    for c in range(channels):
        full = rows_of(cot_ref, c)
        cots.append([full[:, q * LANES : (q + 1) * LANES] for q in range(tiles)])
    lane = lax.broadcasted_iota(jnp.int32, (cells, LANES), 1)
    base = lane - lax.rem(lane, NODES)

    def step(n, acc):
        index = base + n
        slab = rows_of(inv_ref, n)
        out = []
        for c in range(channels):
            for q in range(tiles):
                spread = jnp.take_along_axis(cots[c][q], index, axis=1, mode="promise_in_bounds")
                out.append(acc[c * tiles + q] + slab[:, q * LANES : (q + 1) * LANES] * spread)
        return tuple(out)

    zero = jnp.zeros((cells, LANES), F32)
    acc = lax.fori_loop(0, NODES, step, (zero,) * (channels * tiles), unroll=4)
    ones = jnp.ones((cells, line), F32)
    blank = jnp.zeros((cells, line), F32)

    def fill(get):
        for r in range(GROUP):
            value = get(r) if r < channels else (ones if r == channels else blank)
            for q in range(tiles):
                rows_ref[q, pl.ds(r, cells, stride=GROUP), :] = value[:, q * LANES : (q + 1) * LANES]

    def tile_of(t):
        return jnp.concatenate([rows_ref[q, t * GROUP : (t + 1) * GROUP, :] for q in range(tiles)], axis=1)

    adjoint = [jnp.concatenate(acc[c * tiles : (c + 1) * tiles], axis=1) for c in range(channels)]
    for c in range(channels):
        adj_ref[c] = adjoint[c]
        left_ref[c] = adjoint[c][:span]
        right_ref[c] = adjoint[c][span:]
        front_ref[c] = jnp.concatenate([adjoint[c][0:1], adjoint[c][span : span + 1]], axis=0)
        back_ref[c] = jnp.concatenate([adjoint[c][span - 1 : span], adjoint[c][cells - 1 :]], axis=0)
    fill(lambda r: DT_STEP * adjoint[r])
    for t in range(cells):
        tile = tile_of(t)
        og_ref[t] = jnp.concatenate([tile, blank], axis=0).astype(BF16)
    fill(lambda r: rows_of(state_ref, r))
    for t in range(cells):
        tile = tile_of(t)
        high = tile.astype(BF16).astype(F32)
        xs_ref[t] = jnp.concatenate([high, tile - high, high, blank], axis=0).astype(BF16)
    w_mid_t_ref[...] = w_mid_ref[...].astype(F32).T.astype(BF16)
    b_col_ref[...] = jnp.broadcast_to(b_mid_ref[...], (LANES, b_mid_ref.shape[1])).T


def dot(a, b):
    return jnp.dot(a, b, preferred_element_type=F32)


def dot_nt(a, b):
    return lax.dot_general(a, b, (((1,), (1,)), ((), ())), preferred_element_type=F32)


def sigmoid(v):
    return 0.5 * jnp.tanh(0.5 * v) + 0.5


def closure_kernel(
    entries,
    core_ref, squares_ref, xs_ref, og_ref, w_in_ref, b_in_ref, w_mid_ref, w_mid_t_ref, b_col_ref, w_out_ref,
    back_ref, mine_ref, other_ref,
    mid_ref, in_ref, out_ref,
):
    cells = xs_ref.shape[0]
    channels, hidden = w_in_ref.shape
    total = jnp.sum(squares_ref[...], axis=0, keepdims=True)
    inv_norm = lax.rsqrt(total / entries + EPS)[:, :1]
    weights = jnp.concatenate(
        [inv_norm * w_in_ref[...], b_in_ref[...], jnp.zeros((GROUP - channels - 1, hidden), F32)], axis=0
    )
    high = weights.astype(BF16).astype(F32)
    low = weights - high
    pair = jnp.concatenate([high, low], axis=0).astype(BF16)
    first = jnp.concatenate([high, high, low, jnp.zeros_like(low)], axis=0).T.astype(BF16)
    mid_ref[...] = jnp.zeros_like(mid_ref)
    in_ref[...] = jnp.zeros_like(in_ref)
    out_ref[...] = jnp.zeros_like(out_ref)

    def step(t, carry):
        x = xs_ref[t]
        og = og_ref[t]
        pre_first = dot(first, x)
        gate = sigmoid(pre_first)
        act = pre_first * gate
        slope_one = gate + act * (1.0 - gate)
        hidden_one = act.astype(BF16)
        pre_second = dot(w_mid_t_ref[...], hidden_one) + b_col_ref[:, :1]
        gate = sigmoid(pre_second)
        act = pre_second * gate
        slope_two = gate + act * (1.0 - gate)
        hidden_two = act.astype(BF16)
        delta_two = (dot(w_out_ref[...], og) * slope_two).astype(BF16)
        delta_one = (dot(w_mid_ref[...], delta_two) * slope_one).astype(BF16)
        mid_ref[...] += dot_nt(jnp.concatenate([hidden_one, og], axis=0), delta_two)
        out_ref[...] += dot_nt(og, hidden_two)
        in_ref[...] += dot_nt(x[: 2 * GROUP], delta_one)
        back = dot(pair, delta_one)
        back = back[:GROUP] + back[GROUP:]
        place = pl.ds(pl.multiple_of(t * GROUP, GROUP), GROUP)
        for q in range(back_ref.shape[0]):
            back_ref[q, place, :] = back[:, q * LANES : (q + 1) * LANES]
        return carry

    lax.fori_loop(0, cells, step, 0)
    c = channels
    sums = in_ref[...]
    extra = jnp.concatenate(
        [
            (sums[:c] + sums[GROUP : GROUP + c]) * inv_norm,
            sums[c : c + 1],
            jnp.zeros((GROUP - c - 1, hidden), F32),
            out_ref[:c],
            mid_ref[hidden + c : hidden + c + 1],
            jnp.zeros((GROUP - c - 1, hidden), F32),
        ],
        axis=0,
    )
    half = hidden // 2
    wide = jnp.concatenate([extra[:, :half], extra[:, half:]], axis=0)
    wide = jnp.concatenate([wide, jnp.zeros((half - wide.shape[0], half), F32)], axis=0)
    core = core_ref[0]
    own = pl.multiple_of(core * half, half)
    away = pl.multiple_of((1 - core) * half, half)
    mine_ref[:, 0, :hidden] = mid_ref[pl.ds(own, half), :]
    other_ref[:, 0, :hidden] = mid_ref[pl.ds(away, half), :]
    first_half = core == 0
    mine_ref[:, 0, hidden:] = jnp.where(first_half, wide, 0.0)
    other_ref[:, 0, hidden:] = jnp.where(first_half, 0.0, wide)


def finish_kernel(
    tags_ref, adj_ref, back_ref, left_ref, right_ref, front_ref, rear_ref, out_ref
):
    channels, cells, line = adj_ref.shape
    span = cells // 2
    lane = lax.broadcasted_iota(jnp.int32, (cells, line), 1)
    row = lax.broadcasted_iota(jnp.int32, (cells, line), 0)
    node = lax.rem(lane, NODES)
    a, b, c3 = node // 16, lax.rem(node // 4, 4), lax.rem(node, 4)
    bottom = jnp.zeros((cells, line), F32)
    top = jnp.zeros((cells, line), F32)
    for r in range(cells):
        bottom = jnp.where(row == r, 1.0 - 2.0 * tags_ref[0, r].astype(F32), bottom)
        top = jnp.where(row == r, 1.0 - 2.0 * tags_ref[1, r].astype(F32), top)
    low_wall = lane < NODES
    high_wall = lane >= line - NODES
    for c in range(channels):
        v = adj_ref[c]
        lx = jnp.concatenate([left_ref[c], v[:span]], axis=0)
        ux = jnp.concatenate([v[span:], right_ref[c]], axis=0)
        lz = jnp.concatenate([front_ref[c, 0:1], v[: span - 1], front_ref[c, 1:2], v[span : cells - 1]], axis=0)
        uz = jnp.concatenate([v[1:span], rear_ref[c, 0:1], v[span + 1 :], rear_ref[c, 1:2]], axis=0)
        ly = jnp.where(low_wall, bottom * v, pltpu.roll(v, 52, 1))
        uy = jnp.where(high_wall, top * v, pltpu.roll(v, line - 52, 1))
        jump = jnp.where(a == 0, pltpu.roll(lx, line - 48, 1) - v, 0.0)
        jump += jnp.where(a == 3, pltpu.roll(ux, 48, 1) - v, 0.0)
        jump += jnp.where(b == 0, ly - v, 0.0)
        jump += jnp.where(b == 3, uy - v, 0.0)
        jump += jnp.where(c3 == 0, pltpu.roll(lz, line - 3, 1) - v, 0.0)
        jump += jnp.where(c3 == 3, pltpu.roll(uz, 3, 1) - v, 0.0)
        back = jnp.concatenate(
            [back_ref[q, pl.ds(c, cells, stride=GROUP), :] for q in range(line // LANES)], axis=1
        )
        total = v + (0.5 * KAPPA) * jump + back
        out_ref[c, 0] = total[:span]
        out_ref[c, 1] = total[span:]


def shape(*dims, dtype=F32):
    return jax.ShapeDtypeStruct(dims, dtype)


def run_adjoint(state, cotangent, local_inverse, w_mid, b_mid):
    channels, _, span, line = state.shape
    cells = 2 * span
    hidden = w_mid.shape[0]
    return pl.pallas_call(
        adjoint_kernel,
        out_shape=(
            shape(channels, cells, line),
            shape(cells, 2 * GROUP, line, dtype=BF16),
            shape(cells, 4 * GROUP, line, dtype=BF16),
            shape(hidden, hidden, dtype=BF16),
            shape(hidden, LANES),
            shape(channels, span, line),
            shape(channels, span, line),
            shape(channels, 2, line),
            shape(channels, 2, line),
        ),
        in_specs=whole_vmem(5),
        out_specs=tuple(whole_vmem(9)),
        scratch_shapes=[pltpu.VMEM((line // LANES, cells * GROUP, LANES), F32)],
        name="adjoint",
    )(state, cotangent, local_inverse, w_mid, b_mid.reshape(1, hidden))


def run_closure(entries, core, squares, xs, og, w_in, b_in, w_mid, w_mid_t, b_col, w_out):
    cells, _, line = xs.shape
    channels, hidden = w_in.shape
    half = hidden // 2
    return pl.pallas_call(
        functools.partial(closure_kernel, entries),
        out_shape=(
            shape(line // LANES, cells * GROUP, LANES),
            shape(half, 1, hidden + LANES),
            shape(half, 1, hidden + LANES),
        ),
        in_specs=[pl.BlockSpec(memory_space=pltpu.SMEM)] + whole_vmem(9),
        out_specs=tuple(whole_vmem(3)),
        scratch_shapes=[
            pltpu.VMEM((hidden + 2 * GROUP, hidden), F32),
            pltpu.VMEM((2 * GROUP, hidden), F32),
            pltpu.VMEM((2 * GROUP, hidden), F32),
        ],
        name="closure",
    )(core, squares, xs, og, w_in, b_in.reshape(1, hidden), w_mid, w_mid_t, b_col, w_out)


def run_finish(tags, adjoint, back, left, right, front, rear):
    channels, cells, line = adjoint.shape
    return pl.pallas_call(
        finish_kernel,
        out_shape=shape(channels, 2, cells // 2, line),
        in_specs=[pl.BlockSpec(memory_space=pltpu.SMEM)] + whole_vmem(6),
        out_specs=pl.BlockSpec(memory_space=pltpu.VMEM),
        name="finish",
    )(tags, adjoint, back, left, right, front, rear)


def ring(count, step):
    return [(i, (i + step) % count) for i in range(count)]


def exchange(value, axes):
    return lax.all_to_all(value, axes, 0, 0, tiled=True)


def per_device(state, cotangent, local_inverse, wall_tags, w_in, b_in, w_mid, b_mid, w_out):
    channels, x_elems, z_elems, line = state.shape
    gx, gz = lax.axis_size(GX), lax.axis_size(GZ)
    devices = gx * gz
    chips = devices // 2
    nodes = x_elems * z_elems * line * devices
    hidden = w_mid.shape[0]
    swap = [(0, 1), (1, 0)]
    core = lax.axis_index("core")

    squares = jnp.broadcast_to(jnp.sum(state * state), (devices, 1, LANES))
    squares = exchange(squares, AXES).reshape(devices, LANES)
    adjoint, og, xs, w_mid_t, b_col, low_x, high_x, low_z, high_z = run_adjoint(
        state, cotangent, local_inverse, w_mid, b_mid
    )
    from_left = lax.ppermute(high_x, GX, ring(gx, 1))
    from_right = lax.ppermute(low_x, GX, ring(gx, -1))
    from_front = lax.ppermute(high_z, GZ, ring(gz, 1))
    from_rear = lax.ppermute(low_z, GZ, ring(gz, -1))
    w_out_wide = jnp.pad(w_out, ((0, 0), (0, 2 * GROUP - channels)))
    back, mine, other = run_closure(
        float(channels * nodes), core.reshape(1), squares, xs, og, w_in, b_in, w_mid, w_mid_t, b_col, w_out_wide
    )
    mine = mine + lax.ppermute(other, "core", swap)
    factor = 4.0 / math.sqrt(nodes)
    chunk = factor * jnp.sum(exchange(mine, CHIPS), axis=0, keepdims=True)
    gathered = exchange(jnp.broadcast_to(chunk, (chips,) + chunk.shape[1:]), CHIPS)
    partner = lax.ppermute(gathered, "core", swap)
    grad_state = run_finish(
        wall_tags.reshape(2, x_elems * z_elems), adjoint, back, from_left, from_right, from_front, from_rear
    )
    gathered, partner = gathered[:, 0], partner[:, 0]
    first = jnp.where(core == 0, gathered, partner)
    second = jnp.where(core == 0, partner, gathered)
    grad_mid = jnp.concatenate([first[:, :hidden], second[:, :hidden]], axis=0)
    extra = jnp.concatenate([first[: 2 * GROUP, hidden:], first[2 * GROUP : 4 * GROUP, hidden:]], axis=1)
    c = channels
    return (
        grad_state,
        extra[:c],
        extra[c],
        grad_mid,
        extra[GROUP + c],
        extra[GROUP : GROUP + c].T,
    )


def solution(mesh):
    fine = Mesh(mesh.devices.reshape(2, 4, 4, 4, 2), AXES)
    block = P(None, GX, GZ, None)
    placed = (block, block, block, P(None, GX, GZ)) + (P(),) * 5
    return jax.shard_map(
        per_device,
        mesh=fine,
        in_specs=placed,
        out_specs=(block, P(), P(), P(), P(), P()),
        check_vma=False,
    )
```

```python
import functools
import math

import jax
import jax.numpy as jnp
from jax import lax
from jax.experimental import pallas as pl
from jax.experimental.pallas import tpu as pltpu
from jax.sharding import Mesh, PartitionSpec as P

KAPPA = 0.5
DT_STEP = 0.5
EPS = 1e-06

AXES = ("zhi", "y", "x", "zlo", "core")
GX = ("zhi", "y")
GZ = ("x", "zlo", "core")
PLANE = ("y", "x")
COLUMN = ("zhi", "zlo", "core")
LANES = 128
NODES = 64
GROUP = 8
F32 = jnp.float32
BF16 = jnp.bfloat16


def whole_vmem(count):
    return [pl.BlockSpec(memory_space=pltpu.VMEM)] * count


def rows_of(ref, *lead):
    return jnp.concatenate([ref[lead + (0,)], ref[lead + (1,)]], axis=0)


def squares_kernel(state_ref, out_ref):
    total = jnp.zeros((2 * state_ref.shape[2], state_ref.shape[3]), F32)
    for c in range(state_ref.shape[0]):
        value = rows_of(state_ref, c)
        total += value * value
    out_ref[...] = jnp.broadcast_to(jnp.sum(total, keepdims=True), out_ref.shape)


def adjoint_kernel(
    state_ref, cot_ref, inv_ref, w_mid_ref, b_mid_ref, w_out_ref,
    adj_ref, og_ref, xs_ref, w_mid_t_ref, b_col_ref, w_wide_ref, left_ref, right_ref, front_ref, back_ref,
    rows_ref,
):
    channels, _, span, line = state_ref.shape
    tiles = line // LANES
    cells = 2 * span
    cots = []
    for c in range(channels):
        full = rows_of(cot_ref, c)
        cots.append([full[:, q * LANES : (q + 1) * LANES] for q in range(tiles)])
    lane = lax.broadcasted_iota(jnp.int32, (cells, LANES), 1)
    base = lane - lax.rem(lane, NODES)

    def step(n, acc):
        index = base + n
        slab = rows_of(inv_ref, n)
        out = []
        for c in range(channels):
            for q in range(tiles):
                spread = jnp.take_along_axis(cots[c][q], index, axis=1, mode="promise_in_bounds")
                out.append(acc[c * tiles + q] + slab[:, q * LANES : (q + 1) * LANES] * spread)
        return tuple(out)

    zero = jnp.zeros((cells, LANES), F32)
    acc = lax.fori_loop(0, NODES, step, (zero,) * (channels * tiles), unroll=4)
    ones = jnp.ones((cells, line), F32)
    blank = jnp.zeros((cells, line), F32)

    def fill(get):
        for r in range(GROUP):
            value = get(r) if r < channels else (ones if r == channels else blank)
            for q in range(tiles):
                rows_ref[q, pl.ds(r, cells, stride=GROUP), :] = value[:, q * LANES : (q + 1) * LANES]

    def tile_of(t):
        return jnp.concatenate([rows_ref[q, t * GROUP : (t + 1) * GROUP, :] for q in range(tiles)], axis=1)

    adjoint = [jnp.concatenate(acc[c * tiles : (c + 1) * tiles], axis=1) for c in range(channels)]
    for c in range(channels):
        adj_ref[c] = adjoint[c]
        left_ref[c] = adjoint[c][:span]
        right_ref[c] = adjoint[c][span:]
        front_ref[c] = jnp.concatenate([adjoint[c][0:1], adjoint[c][span : span + 1]], axis=0)
        back_ref[c] = jnp.concatenate([adjoint[c][span - 1 : span], adjoint[c][cells - 1 :]], axis=0)
    fill(lambda r: DT_STEP * adjoint[r])
    for t in range(cells):
        tile = tile_of(t)
        og_ref[t] = jnp.concatenate([tile, blank], axis=0).astype(BF16)
    fill(lambda r: rows_of(state_ref, r))
    for t in range(cells):
        tile = tile_of(t)
        high = tile.astype(BF16).astype(F32)
        xs_ref[t] = jnp.concatenate([high, tile - high, high, blank], axis=0).astype(BF16)
    w_mid_t_ref[...] = w_mid_ref[...].astype(F32).T.astype(BF16)
    b_col_ref[...] = jnp.broadcast_to(b_mid_ref[...], (LANES, b_mid_ref.shape[1])).T
    hidden = w_out_ref.shape[0]
    w_wide_ref[...] = jnp.concatenate(
        [w_out_ref[...].astype(F32), jnp.zeros((hidden, 2 * GROUP - channels), F32)], axis=1
    ).astype(BF16)


def dot(a, b):
    return jnp.dot(a, b, preferred_element_type=F32)


def dot_nt(a, b):
    return lax.dot_general(a, b, (((1,), (1,)), ((), ())), preferred_element_type=F32)


def sigmoid(v):
    return 0.5 * jnp.tanh(0.5 * v) + 0.5


def closure_kernel(
    entries,
    core_ref, squares_ref, xs_ref, og_ref, w_in_ref, b_in_ref, w_mid_ref, w_mid_t_ref, b_col_ref, w_out_ref,
    back_ref, mine_ref, other_ref,
    mid_ref, in_ref, out_ref, wide_ref,
):
    cells = xs_ref.shape[0]
    channels, hidden = w_in_ref.shape
    total = jnp.sum(squares_ref[...], axis=0, keepdims=True)
    inv_norm = lax.rsqrt(total / entries + EPS)[:, :1]
    weights = jnp.concatenate(
        [inv_norm * w_in_ref[...], b_in_ref[...], jnp.zeros((GROUP - channels - 1, hidden), F32)], axis=0
    )
    high = weights.astype(BF16).astype(F32)
    low = weights - high
    pair = jnp.concatenate([high, low], axis=0).astype(BF16)
    first = jnp.concatenate([high, high, low, jnp.zeros_like(low)], axis=0).T.astype(BF16)
    mid_ref[...] = jnp.zeros_like(mid_ref)
    in_ref[...] = jnp.zeros_like(in_ref)
    out_ref[...] = jnp.zeros_like(out_ref)

    def step(t, carry):
        x = xs_ref[t]
        og = og_ref[t]
        pre_first = dot(first, x)
        gate = sigmoid(pre_first)
        act = pre_first * gate
        slope_one = gate + act * (1.0 - gate)
        hidden_one = act.astype(BF16)
        pre_second = dot(w_mid_t_ref[...], hidden_one) + b_col_ref[:, :1]
        gate = sigmoid(pre_second)
        act = pre_second * gate
        slope_two = gate + act * (1.0 - gate)
        hidden_two = act.astype(BF16)
        delta_two = (dot(w_out_ref[...], og) * slope_two).astype(BF16)
        delta_one = (dot(w_mid_ref[...], delta_two) * slope_one).astype(BF16)
        mid_ref[...] += dot_nt(jnp.concatenate([hidden_one, og], axis=0), delta_two)
        out_ref[...] += dot_nt(og, hidden_two)
        in_ref[...] += dot_nt(x[: 2 * GROUP], delta_one)
        back = dot(pair, delta_one)
        back = back[:GROUP] + back[GROUP:]
        place = pl.ds(pl.multiple_of(t * GROUP, GROUP), GROUP)
        for q in range(back_ref.shape[0]):
            back_ref[q, place, :] = back[:, q * LANES : (q + 1) * LANES]
        return carry

    lax.fori_loop(0, cells, step, 0)
    c = channels
    sums = in_ref[...]
    extra = jnp.concatenate(
        [
            (sums[:c] + sums[GROUP : GROUP + c]) * inv_norm,
            sums[c : c + 1],
            jnp.zeros((GROUP - c - 1, hidden), F32),
            out_ref[:c],
            mid_ref[hidden + c : hidden + c + 1],
            jnp.zeros((GROUP - c - 1, hidden), F32),
        ],
        axis=0,
    )
    half = hidden // 2
    wide_ref[: 2 * GROUP, :] = extra[:, :half]
    wide_ref[2 * GROUP :, :] = extra[:, half:]
    core = core_ref[0]
    for g in range(hidden // (2 * GROUP)):
        own = pl.multiple_of(g * 2 * GROUP + core * GROUP, GROUP)
        away = pl.multiple_of(g * 2 * GROUP + (1 - core) * GROUP, GROUP)
        for ref, start in ((mine_ref, own), (other_ref, away)):
            ref[g, :, :hidden] = mid_ref[pl.ds(start, GROUP), :]
            if g < 2:
                ref[g, :, hidden:] = wide_ref[pl.ds(start, GROUP), :]
            else:
                ref[g, :, hidden:] = jnp.zeros((GROUP, LANES), F32)


def finish_kernel(
    tags_ref, adj_ref, back_ref, left_ref, right_ref, front_ref, rear_ref, out_ref
):
    channels, cells, line = adj_ref.shape
    span = cells // 2
    lane = lax.broadcasted_iota(jnp.int32, (cells, line), 1)
    row = lax.broadcasted_iota(jnp.int32, (cells, line), 0)
    node = lax.rem(lane, NODES)
    a, b, c3 = node // 16, lax.rem(node // 4, 4), lax.rem(node, 4)
    bottom = jnp.zeros((cells, line), F32)
    top = jnp.zeros((cells, line), F32)
    for r in range(cells):
        bottom = jnp.where(row == r, 1.0 - 2.0 * tags_ref[0, r // span, r % span].astype(F32), bottom)
        top = jnp.where(row == r, 1.0 - 2.0 * tags_ref[1, r // span, r % span].astype(F32), top)
    low_wall = lane < NODES
    high_wall = lane >= line - NODES
    for c in range(channels):
        v = adj_ref[c]
        lx = jnp.concatenate([left_ref[c], v[:span]], axis=0)
        ux = jnp.concatenate([v[span:], right_ref[c]], axis=0)
        lz = jnp.concatenate([front_ref[c, 0:1], v[: span - 1], front_ref[c, 1:2], v[span : cells - 1]], axis=0)
        uz = jnp.concatenate([v[1:span], rear_ref[c, 0:1], v[span + 1 :], rear_ref[c, 1:2]], axis=0)
        ly = jnp.where(low_wall, bottom * v, pltpu.roll(v, 52, 1))
        uy = jnp.where(high_wall, top * v, pltpu.roll(v, line - 52, 1))
        jump = jnp.where(a == 0, pltpu.roll(lx, line - 48, 1) - v, 0.0)
        jump += jnp.where(a == 3, pltpu.roll(ux, 48, 1) - v, 0.0)
        jump += jnp.where(b == 0, ly - v, 0.0)
        jump += jnp.where(b == 3, uy - v, 0.0)
        jump += jnp.where(c3 == 0, pltpu.roll(lz, line - 3, 1) - v, 0.0)
        jump += jnp.where(c3 == 3, pltpu.roll(uz, 3, 1) - v, 0.0)
        back = jnp.concatenate(
            [back_ref[q, pl.ds(c, cells, stride=GROUP), :] for q in range(line // LANES)], axis=1
        )
        total = v + (0.5 * KAPPA) * jump + back
        out_ref[c, 0] = total[:span]
        out_ref[c, 1] = total[span:]


def unpack_kernel(sums_ref, in_ref, b_in_ref, mid_ref, b_mid_ref, out_ref):
    channels, hidden = in_ref.shape
    mid_ref[...] = sums_ref[:, :hidden]
    extra = jnp.concatenate(
        [sums_ref[: 2 * GROUP, hidden:], sums_ref[2 * GROUP : 4 * GROUP, hidden:]], axis=1
    )
    in_ref[...] = extra[:channels]
    b_in_ref[...] = extra[channels : channels + 1]
    b_mid_ref[...] = extra[GROUP + channels : GROUP + channels + 1]
    out_ref[...] = extra[GROUP:].T[:, :channels]


def shape(*dims, dtype=F32):
    return jax.ShapeDtypeStruct(dims, dtype)


def run_squares(state, devices):
    return pl.pallas_call(
        squares_kernel,
        out_shape=shape(devices, LANES),
        in_specs=whole_vmem(1),
        out_specs=whole_vmem(1)[0],
        name="squares",
    )(state)


def run_unpack(sums, channels):
    hidden = sums.shape[0]
    return pl.pallas_call(
        unpack_kernel,
        out_shape=(
            shape(channels, hidden),
            shape(1, hidden),
            shape(hidden, hidden),
            shape(1, hidden),
            shape(hidden, channels),
        ),
        in_specs=whole_vmem(1),
        out_specs=tuple(whole_vmem(5)),
        name="unpack",
    )(sums)


def run_adjoint(state, cotangent, local_inverse, w_mid, b_mid, w_out):
    channels, _, span, line = state.shape
    cells = 2 * span
    hidden = w_mid.shape[0]
    return pl.pallas_call(
        adjoint_kernel,
        out_shape=(
            shape(channels, cells, line),
            shape(cells, 2 * GROUP, line, dtype=BF16),
            shape(cells, 4 * GROUP, line, dtype=BF16),
            shape(hidden, hidden, dtype=BF16),
            shape(hidden, LANES),
            shape(hidden, 2 * GROUP, dtype=BF16),
            shape(channels, span, line),
            shape(channels, span, line),
            shape(channels, 2, line),
            shape(channels, 2, line),
        ),
        in_specs=whole_vmem(6),
        out_specs=tuple(whole_vmem(10)),
        scratch_shapes=[pltpu.VMEM((line // LANES, cells * GROUP, LANES), F32)],
        name="adjoint",
    )(state, cotangent, local_inverse, w_mid, b_mid.reshape(1, hidden), w_out)


def run_closure(entries, core, squares, xs, og, w_in, b_in, w_mid, w_mid_t, b_col, w_out):
    cells, _, line = xs.shape
    channels, hidden = w_in.shape
    return pl.pallas_call(
        functools.partial(closure_kernel, entries),
        out_shape=(
            shape(line // LANES, cells * GROUP, LANES),
            shape(hidden // (2 * GROUP), GROUP, hidden + LANES),
            shape(hidden // (2 * GROUP), GROUP, hidden + LANES),
        ),
        in_specs=[pl.BlockSpec(memory_space=pltpu.SMEM)] + whole_vmem(9),
        out_specs=tuple(whole_vmem(3)),
        scratch_shapes=[
            pltpu.VMEM((hidden + 2 * GROUP, hidden), F32),
            pltpu.VMEM((2 * GROUP, hidden), F32),
            pltpu.VMEM((2 * GROUP, hidden), F32),
            pltpu.VMEM((4 * GROUP, LANES), F32),
        ],
        name="closure",
    )(core, squares, xs, og, w_in, b_in.reshape(1, hidden), w_mid, w_mid_t, b_col, w_out)


def run_finish(tags, adjoint, back, left, right, front, rear):
    channels, cells, line = adjoint.shape
    return pl.pallas_call(
        finish_kernel,
        out_shape=shape(channels, 2, cells // 2, line),
        in_specs=[pl.BlockSpec(memory_space=pltpu.SMEM)] + whole_vmem(6),
        out_specs=pl.BlockSpec(memory_space=pltpu.VMEM),
        name="finish",
    )(tags, adjoint, back, left, right, front, rear)


def ring(count, step):
    return [(i, (i + step) % count) for i in range(count)]


def exchange(value, axes):
    return lax.all_to_all(value, axes, 0, 0, tiled=True)


def per_device(state, cotangent, local_inverse, wall_tags, w_in, b_in, w_mid, b_mid, w_out):
    channels, x_elems, z_elems, line = state.shape
    gx, gz = lax.axis_size(GX), lax.axis_size(GZ)
    devices = gx * gz
    nodes = x_elems * z_elems * line * devices
    swap = [(0, 1), (1, 0)]
    core = lax.axis_index("core")

    squares = exchange(run_squares(state, devices).reshape(devices, 1, LANES), AXES)
    adjoint, og, xs, w_mid_t, b_col, w_wide, low_x, high_x, low_z, high_z = run_adjoint(
        state, cotangent, local_inverse, w_mid, b_mid, w_out
    )
    halo = (
        lax.ppermute(high_x, GX, ring(gx, 1)),
        lax.ppermute(low_x, GX, ring(gx, -1)),
        lax.ppermute(high_z, GZ, ring(gz, 1)),
        lax.ppermute(low_z, GZ, ring(gz, -1)),
    )
    squares, halo = lax.optimization_barrier((squares, halo))
    back, mine, other = run_closure(
        float(channels * nodes), core.reshape(1), squares.reshape(devices, LANES), xs, og, w_in, b_in, w_mid,
        w_mid_t, b_col, w_wide,
    )
    grad_state = run_finish(wall_tags, adjoint, back, *halo)
    mine = mine + lax.ppermute(other, "core", swap)
    factor = 4.0 / math.sqrt(nodes)
    part = jnp.sum(exchange(mine, PLANE), axis=0)
    part = exchange(jnp.broadcast_to(part, (lax.axis_size(COLUMN),) + part.shape), COLUMN)
    part = factor * jnp.sum(part.reshape(-1, 2, *part.shape[1:]), axis=0)
    part = part.reshape(-1, part.shape[-1])
    sums = exchange(jnp.broadcast_to(part, (lax.axis_size(PLANE),) + part.shape), PLANE)
    grad_in, grad_b_in, grad_mid, grad_b_mid, grad_out = run_unpack(
        sums.reshape(-1, sums.shape[-1]), channels
    )
    return grad_state, grad_in, grad_b_in[0], grad_mid, grad_b_mid[0], grad_out


def solution(mesh):
    fine = Mesh(mesh.devices.reshape(2, 4, 4, 4, 2), AXES)
    block = P(None, GX, GZ, None)
    placed = (block, block, block, P(None, GX, GZ)) + (P(),) * 5
    return jax.shard_map(
        per_device,
        mesh=fine,
        in_specs=placed,
        out_specs=(block, P(), P(), P(), P(), P()),
        check_vma=False,
    )
```

```python
import functools
import math

import jax
import jax.numpy as jnp
from jax import lax
from jax.experimental import pallas as pl
from jax.experimental.pallas import tpu as pltpu
from jax.sharding import Mesh, PartitionSpec as P


KAPPA = 0.5
DT_STEP = 0.5
EPS = 1e-06

AXES = ("zhi", "y", "x", "zlo", "core")
GX = ("zhi", "y")
GZ = ("x", "zlo", "core")
PLANE = ("y", "x")
COLUMN = ("zhi", "zlo", "core")
TOWER = ("zhi", "zlo")
LANES = 128
NODES = 64
GROUP = 8
F32 = jnp.float32
BF16 = jnp.bfloat16


def whole_vmem(count):
    return [pl.BlockSpec(memory_space=pltpu.VMEM)] * count


def rows_of(ref, *lead):
    return jnp.concatenate([ref[lead + (0,)], ref[lead + (1,)]], axis=0)


def squares_kernel(state_ref, out_ref):
    total = jnp.zeros((2 * state_ref.shape[2], state_ref.shape[3]), F32)
    for c in range(state_ref.shape[0]):
        value = rows_of(state_ref, c)
        total += value * value
    out_ref[...] = jnp.broadcast_to(jnp.sum(total, keepdims=True), out_ref.shape)


def adjoint_kernel(
    state_ref, cot_ref, inv_ref, w_mid_ref, b_mid_ref, w_out_ref,
    adj_ref, og_ref, xs_ref, w_mid_t_ref, b_col_ref, w_wide_ref, left_ref, right_ref, front_ref, back_ref,
    rows_ref,
):
    channels, _, span, line = state_ref.shape
    tiles = line // LANES
    cells = 2 * span
    cots = []
    for c in range(channels):
        full = rows_of(cot_ref, c)
        cots.append([full[:, q * LANES : (q + 1) * LANES] for q in range(tiles)])
    lane = lax.broadcasted_iota(jnp.int32, (cells, LANES), 1)
    base = lane - lax.rem(lane, NODES)

    def step(n, acc):
        index = base + n
        slab = rows_of(inv_ref, n)
        out = []
        for c in range(channels):
            for q in range(tiles):
                spread = jnp.take_along_axis(cots[c][q], index, axis=1, mode="promise_in_bounds")
                out.append(acc[c * tiles + q] + slab[:, q * LANES : (q + 1) * LANES] * spread)
        return tuple(out)

    zero = jnp.zeros((cells, LANES), F32)
    acc = lax.fori_loop(0, NODES, step, (zero,) * (channels * tiles), unroll=4)
    ones = jnp.ones((cells, line), F32)
    blank = jnp.zeros((cells, line), F32)

    def fill(get):
        for r in range(GROUP):
            value = get(r) if r < channels else (ones if r == channels else blank)
            for q in range(tiles):
                rows_ref[q, pl.ds(r, cells, stride=GROUP), :] = value[:, q * LANES : (q + 1) * LANES]

    def tile_of(t):
        return jnp.concatenate([rows_ref[q, t * GROUP : (t + 1) * GROUP, :] for q in range(tiles)], axis=1)

    adjoint = [jnp.concatenate(acc[c * tiles : (c + 1) * tiles], axis=1) for c in range(channels)]
    for c in range(channels):
        adj_ref[c] = adjoint[c]
        left_ref[c] = adjoint[c][:span]
        right_ref[c] = adjoint[c][span:]
        front_ref[c] = jnp.concatenate([adjoint[c][0:1], adjoint[c][span : span + 1]], axis=0)
        back_ref[c] = jnp.concatenate([adjoint[c][span - 1 : span], adjoint[c][cells - 1 :]], axis=0)
    fill(lambda r: DT_STEP * adjoint[r])
    for t in range(cells):
        tile = tile_of(t)
        og_ref[t] = jnp.concatenate([tile, blank], axis=0).astype(BF16)
    fill(lambda r: rows_of(state_ref, r))
    for t in range(cells):
        tile = tile_of(t)
        high = tile.astype(BF16).astype(F32)
        xs_ref[t] = jnp.concatenate([high, tile - high, high, blank], axis=0).astype(BF16)
    w_mid_t_ref[...] = w_mid_ref[...].astype(F32).T.astype(BF16)
    b_col_ref[...] = jnp.broadcast_to(b_mid_ref[...], (LANES, b_mid_ref.shape[1])).T
    hidden = w_out_ref.shape[1]
    w_wide_ref[...] = jnp.concatenate(
        [w_out_ref[...].astype(F32), jnp.zeros((2 * GROUP - channels, hidden), F32)], axis=0
    ).T.astype(BF16)


def dot(a, b):
    return jnp.dot(a, b, preferred_element_type=F32)


def dot_nt(a, b):
    return lax.dot_general(a, b, (((1,), (1,)), ((), ())), preferred_element_type=F32)


def sigmoid(v):
    return 0.5 * jnp.tanh(0.5 * v) + 0.5


def closure_kernel(
    entries,
    core_ref, squares_ref, xs_ref, og_ref, w_in_ref, b_in_ref, w_mid_ref, w_mid_t_ref, b_col_ref, w_out_ref,
    back_ref, mine_ref, other_ref,
    mid_ref, in_ref, out_ref, wide_ref,
):
    cells = xs_ref.shape[0]
    channels, hidden = w_in_ref.shape
    total = jnp.sum(squares_ref[...], axis=0, keepdims=True)
    inv_norm = lax.rsqrt(total / entries + EPS)[:, :1]
    weights = jnp.concatenate(
        [inv_norm * w_in_ref[...], b_in_ref[...], jnp.zeros((GROUP - channels - 1, hidden), F32)], axis=0
    )
    high = weights.astype(BF16).astype(F32)
    low = weights - high
    pair = jnp.concatenate([high, low], axis=0).astype(BF16)
    first = jnp.concatenate([high, high, low, jnp.zeros_like(low)], axis=0).T.astype(BF16)
    mid_ref[...] = jnp.zeros_like(mid_ref)
    in_ref[...] = jnp.zeros_like(in_ref)
    out_ref[...] = jnp.zeros_like(out_ref)

    def step(t, carry):
        x = xs_ref[t]
        og = og_ref[t]
        pre_first = dot(first, x)
        gate = sigmoid(pre_first)
        act = pre_first * gate
        slope_one = gate + act * (1.0 - gate)
        hidden_one = act.astype(BF16)
        pre_second = dot(w_mid_t_ref[...], hidden_one) + b_col_ref[:, :1]
        gate = sigmoid(pre_second)
        act = pre_second * gate
        slope_two = gate + act * (1.0 - gate)
        hidden_two = act.astype(BF16)
        delta_two = (dot(w_out_ref[...], og) * slope_two).astype(BF16)
        delta_one = (dot(w_mid_ref[...], delta_two) * slope_one).astype(BF16)
        mid_ref[...] += dot_nt(jnp.concatenate([hidden_one, og], axis=0), delta_two)
        out_ref[...] += dot_nt(og, hidden_two)
        in_ref[...] += dot_nt(x[: 2 * GROUP], delta_one)
        back = dot(pair, delta_one)
        back = back[:GROUP] + back[GROUP:]
        place = pl.ds(pl.multiple_of(t * GROUP, GROUP), GROUP)
        for q in range(back_ref.shape[0]):
            back_ref[q, place, :] = back[:, q * LANES : (q + 1) * LANES]
        return carry

    lax.fori_loop(0, cells, step, 0)
    c = channels
    sums = in_ref[...]
    extra = jnp.concatenate(
        [
            (sums[:c] + sums[GROUP : GROUP + c]) * inv_norm,
            sums[c : c + 1],
            jnp.zeros((GROUP - c - 1, hidden), F32),
            out_ref[:c],
            mid_ref[hidden + c : hidden + c + 1],
            jnp.zeros((GROUP - c - 1, hidden), F32),
        ],
        axis=0,
    )
    half = hidden // 2
    wide_ref[0] = extra[:, :half]
    wide_ref[1] = extra[:, half:]
    core = core_ref[0]
    for ref, place in ((mine_ref, core), (other_ref, 1 - core)):
        start = pl.multiple_of(place * half, half)
        ref[:half, :] = mid_ref[pl.ds(start, half), :half]
        ref[half:hidden, :] = mid_ref[pl.ds(start, half), half:]
        ref[hidden:, :] = wide_ref[place]


def finish_kernel(
    tags_ref, adj_ref, back_ref, left_ref, right_ref, front_ref, rear_ref, out_ref
):
    channels, cells, line = adj_ref.shape
    span = cells // 2
    lane = lax.broadcasted_iota(jnp.int32, (cells, line), 1)
    row = lax.broadcasted_iota(jnp.int32, (cells, line), 0)
    node = lax.rem(lane, NODES)
    a, b, c3 = node // 16, lax.rem(node // 4, 4), lax.rem(node, 4)
    bottom = jnp.zeros((cells, line), F32)
    top = jnp.zeros((cells, line), F32)
    for r in range(cells):
        bottom = jnp.where(row == r, 1.0 - 2.0 * tags_ref[0, r // span, r % span].astype(F32), bottom)
        top = jnp.where(row == r, 1.0 - 2.0 * tags_ref[1, r // span, r % span].astype(F32), top)
    low_wall = lane < NODES
    high_wall = lane >= line - NODES
    for c in range(channels):
        v = adj_ref[c]
        lx = jnp.concatenate([left_ref[c], v[:span]], axis=0)
        ux = jnp.concatenate([v[span:], right_ref[c]], axis=0)
        lz = jnp.concatenate([front_ref[c, 0:1], v[: span - 1], front_ref[c, 1:2], v[span : cells - 1]], axis=0)
        uz = jnp.concatenate([v[1:span], rear_ref[c, 0:1], v[span + 1 :], rear_ref[c, 1:2]], axis=0)
        ly = jnp.where(low_wall, bottom * v, pltpu.roll(v, 52, 1))
        uy = jnp.where(high_wall, top * v, pltpu.roll(v, line - 52, 1))
        jump = jnp.where(a == 0, pltpu.roll(lx, line - 48, 1) - v, 0.0)
        jump += jnp.where(a == 3, pltpu.roll(ux, 48, 1) - v, 0.0)
        jump += jnp.where(b == 0, ly - v, 0.0)
        jump += jnp.where(b == 3, uy - v, 0.0)
        jump += jnp.where(c3 == 0, pltpu.roll(lz, line - 3, 1) - v, 0.0)
        jump += jnp.where(c3 == 3, pltpu.roll(uz, 3, 1) - v, 0.0)
        back = jnp.concatenate(
            [back_ref[q, pl.ds(c, cells, stride=GROUP), :] for q in range(line // LANES)], axis=1
        )
        total = v + (0.5 * KAPPA) * jump + back
        out_ref[c, 0] = total[:span]
        out_ref[c, 1] = total[span:]


def unpack_kernel(core_ref, own_ref, away_ref, in_ref, b_in_ref, mid_ref, b_mid_ref, out_ref):
    channels, hidden = in_ref.shape
    half = hidden // 2
    own, away = own_ref[...], away_ref[...]
    first = jnp.where(core_ref[0] == 0, own, away)
    second = jnp.where(core_ref[0] == 0, away, own)
    for k, part in enumerate((first, second)):
        mid_ref[k * half : (k + 1) * half, :half] = part[:half]
        mid_ref[k * half : (k + 1) * half, half:] = part[half:hidden]
    extra = jnp.concatenate([first[hidden:], second[hidden:]], axis=1)
    in_ref[...] = extra[:channels]
    b_in_ref[...] = extra[channels : channels + 1]
    out_ref[...] = extra[GROUP : GROUP + channels]
    b_mid_ref[...] = extra[GROUP + channels : GROUP + channels + 1]


def shape(*dims, dtype=F32):
    return jax.ShapeDtypeStruct(dims, dtype)


def run_squares(state, peers):
    return pl.pallas_call(
        squares_kernel,
        out_shape=shape(peers, LANES),
        in_specs=whole_vmem(1),
        out_specs=whole_vmem(1)[0],
        name="squares",
    )(state)


def run_unpack(core, own, away, channels):
    hidden = own.shape[0] - 2 * GROUP
    return pl.pallas_call(
        unpack_kernel,
        out_shape=(
            shape(channels, hidden),
            shape(1, hidden),
            shape(hidden, hidden),
            shape(1, hidden),
            shape(channels, hidden),
        ),
        in_specs=[pl.BlockSpec(memory_space=pltpu.SMEM)] + whole_vmem(2),
        out_specs=tuple(whole_vmem(5)),
        name="unpack",
    )(core, own, away)


def run_adjoint(state, cotangent, local_inverse, w_mid, b_mid, w_out):
    channels, _, span, line = state.shape
    cells = 2 * span
    hidden = w_mid.shape[0]
    return pl.pallas_call(
        adjoint_kernel,
        out_shape=(
            shape(channels, cells, line),
            shape(cells, 2 * GROUP, line, dtype=BF16),
            shape(cells, 4 * GROUP, line, dtype=BF16),
            shape(hidden, hidden, dtype=BF16),
            shape(hidden, LANES),
            shape(hidden, 2 * GROUP, dtype=BF16),
            shape(channels, span, line),
            shape(channels, span, line),
            shape(channels, 2, line),
            shape(channels, 2, line),
        ),
        in_specs=whole_vmem(6),
        out_specs=tuple(whole_vmem(10)),
        scratch_shapes=[pltpu.VMEM((line // LANES, cells * GROUP, LANES), F32)],
        name="adjoint",
    )(state, cotangent, local_inverse, w_mid, b_mid.reshape(1, hidden), w_out.T)


def run_closure(entries, core, squares, xs, og, w_in, b_in, w_mid, w_mid_t, b_col, w_out):
    cells, _, line = xs.shape
    _, hidden = w_in.shape
    return pl.pallas_call(
        functools.partial(closure_kernel, entries),
        out_shape=(
            shape(line // LANES, cells * GROUP, LANES),
            shape(hidden + 2 * GROUP, LANES),
            shape(hidden + 2 * GROUP, LANES),
        ),
        in_specs=[pl.BlockSpec(memory_space=pltpu.SMEM)] + whole_vmem(9),
        out_specs=tuple(whole_vmem(3)),
        scratch_shapes=[
            pltpu.VMEM((hidden + 2 * GROUP, hidden), F32),
            pltpu.VMEM((2 * GROUP, hidden), F32),
            pltpu.VMEM((2 * GROUP, hidden), F32),
            pltpu.VMEM((2, 2 * GROUP, LANES), F32),
        ],
        name="closure",
    )(core, squares, xs, og, w_in, b_in.reshape(1, hidden), w_mid, w_mid_t, b_col, w_out)


def run_finish(tags, adjoint, back, left, right, front, rear):
    channels, cells, line = adjoint.shape
    return pl.pallas_call(
        finish_kernel,
        out_shape=shape(channels, 2, cells // 2, line),
        in_specs=[pl.BlockSpec(memory_space=pltpu.SMEM)] + whole_vmem(6),
        out_specs=pl.BlockSpec(memory_space=pltpu.VMEM),
        name="finish",
    )(tags, adjoint, back, left, right, front, rear)


def ring(count, step):
    return [(i, (i + step) % count) for i in range(count)]


def exchange(value, axes):
    return lax.all_to_all(value, axes, 0, 0, tiled=True)


def per_device(state, cotangent, local_inverse, wall_tags, w_in, b_in, w_mid, b_mid, w_out):
    channels, x_elems, z_elems, line = state.shape
    gx, gz = lax.axis_size(GX), lax.axis_size(GZ)
    devices = gx * gz
    nodes = x_elems * z_elems * line * devices
    swap = [(0, 1), (1, 0)]
    core = lax.axis_index("core")

    plane, column, tower = lax.axis_size(PLANE), lax.axis_size(COLUMN), lax.axis_size(TOWER)
    squares = run_squares(state, plane).reshape(plane, 1, LANES)
    squares = exchange(squares, PLANE)
    squares = jnp.broadcast_to(jnp.sum(squares, axis=0, keepdims=True), (column, 1, LANES))
    squares = exchange(squares, COLUMN)
    adjoint, og, xs, w_mid_t, b_col, w_wide, low_x, high_x, low_z, high_z = run_adjoint(
        state, cotangent, local_inverse, w_mid, b_mid, w_out
    )
    sends = ((high_x, GX, gx, 1), (low_x, GX, gx, -1), (high_z, GZ, gz, 1), (low_z, GZ, gz, -1))
    halo = []
    for face, axes, count, way in sends:
        halo.append(lax.ppermute(face, axes, ring(count, way)))
    core = core.reshape(1)
    back, mine, other = run_closure(
        float(channels * nodes), core, squares.reshape(column, LANES), xs, og, w_in, b_in, w_mid,
        w_mid_t, b_col, w_wide,
    )
    grad_state = run_finish(wall_tags, adjoint, back, *halo)
    mine = mine + lax.ppermute(other, "core", swap)
    factor = 4.0 / math.sqrt(nodes)
    width = mine.shape[0] // plane
    part = exchange(mine.reshape(plane, width, 1, LANES), PLANE)
    part = jnp.broadcast_to(jnp.sum(part, axis=0, keepdims=True), (tower, width, 1, LANES))
    part = exchange(part, TOWER)
    part = jnp.broadcast_to(factor * jnp.sum(part, axis=0, keepdims=True), (plane, width, 1, LANES))
    own = exchange(part, PLANE).reshape(mine.shape)
    away = lax.ppermute(own, "core", swap)
    grad_in, grad_b_in, grad_mid, grad_b_mid, grad_out = run_unpack(core, own, away, channels)
    return grad_state, grad_in, grad_b_in[0], grad_mid, grad_b_mid[0], grad_out.T


def solution(mesh):
    fine = Mesh(mesh.devices.reshape(2, 4, 4, 4, 2), AXES)
    block = P(None, GX, GZ, None)
    placed = (block, block, block, P(None, GX, GZ)) + (P(),) * 5
    return jax.shard_map(
        per_device,
        mesh=fine,
        in_specs=placed,
        out_specs=(block, P(), P(), P(), P(), P()),
        check_vma=False,
    )
```

```python
import functools
import math

import jax
import jax.numpy as jnp
from jax import lax
from jax.experimental import pallas as pl
from jax.experimental.pallas import tpu as pltpu
from jax.sharding import Mesh, PartitionSpec as P


KAPPA = 0.5
DT_STEP = 0.5
EPS = 1e-06

AXES = ("zhi", "y", "x", "zlo", "core")
GX = ("zhi", "y")
GZ = ("x", "zlo", "core")
PLANE = ("y", "x", "core")
TOWER = ("zhi", "zlo")
LANES = 128
NODES = 64
GROUP = 8
F32 = jnp.float32
BF16 = jnp.bfloat16


def whole_vmem(count):
    return [pl.BlockSpec(memory_space=pltpu.VMEM)] * count


def rows_of(ref, *lead):
    return jnp.concatenate([ref[lead + (0,)], ref[lead + (1,)]], axis=0)


def squares_kernel(state_ref, out_ref):
    total = jnp.zeros((2 * state_ref.shape[2], state_ref.shape[3]), F32)
    for c in range(state_ref.shape[0]):
        value = rows_of(state_ref, c)
        total += value * value
    out_ref[...] = jnp.broadcast_to(jnp.sum(total, keepdims=True), out_ref.shape)


def adjoint_kernel(
    state_ref, cot_ref, inv_ref, w_mid_ref, b_mid_ref, w_out_ref,
    adj_ref, og_ref, xs_ref, w_mid_t_ref, b_col_ref, w_wide_ref, left_ref, right_ref, front_ref, back_ref,
    rows_ref,
):
    channels, _, span, line = state_ref.shape
    tiles = line // LANES
    cells = 2 * span
    cots = []
    for c in range(channels):
        full = rows_of(cot_ref, c)
        cots.append([full[:, q * LANES : (q + 1) * LANES] for q in range(tiles)])
    lane = lax.broadcasted_iota(jnp.int32, (cells, LANES), 1)
    base = lane - lax.rem(lane, NODES)

    def step(n, acc):
        index = base + n
        slab = rows_of(inv_ref, n)
        out = []
        for c in range(channels):
            for q in range(tiles):
                spread = jnp.take_along_axis(cots[c][q], index, axis=1, mode="promise_in_bounds")
                out.append(acc[c * tiles + q] + slab[:, q * LANES : (q + 1) * LANES] * spread)
        return tuple(out)

    zero = jnp.zeros((cells, LANES), F32)
    acc = lax.fori_loop(0, NODES, step, (zero,) * (channels * tiles), unroll=4)
    ones = jnp.ones((cells, line), F32)
    blank = jnp.zeros((cells, line), F32)

    def fill(get):
        for r in range(GROUP):
            value = get(r) if r < channels else (ones if r == channels else blank)
            for q in range(tiles):
                rows_ref[q, pl.ds(r, cells, stride=GROUP), :] = value[:, q * LANES : (q + 1) * LANES]

    def tile_of(t):
        return jnp.concatenate([rows_ref[q, t * GROUP : (t + 1) * GROUP, :] for q in range(tiles)], axis=1)

    adjoint = [jnp.concatenate(acc[c * tiles : (c + 1) * tiles], axis=1) for c in range(channels)]
    for c in range(channels):
        adj_ref[c] = adjoint[c]
        left_ref[c] = adjoint[c][:span]
        right_ref[c] = adjoint[c][span:]
        front_ref[c] = jnp.concatenate([adjoint[c][0:1], adjoint[c][span : span + 1]], axis=0)
        back_ref[c] = jnp.concatenate([adjoint[c][span - 1 : span], adjoint[c][cells - 1 :]], axis=0)
    fill(lambda r: DT_STEP * adjoint[r])
    for t in range(cells):
        tile = tile_of(t)
        og_ref[t] = jnp.concatenate([tile, blank], axis=0).astype(BF16)
    fill(lambda r: rows_of(state_ref, r))
    for t in range(cells):
        tile = tile_of(t)
        high = tile.astype(BF16).astype(F32)
        xs_ref[t] = jnp.concatenate([high, tile - high, high, blank], axis=0).astype(BF16)
    w_mid_t_ref[...] = w_mid_ref[...].astype(F32).T.astype(BF16)
    b_col_ref[...] = jnp.broadcast_to(b_mid_ref[...], (LANES, b_mid_ref.shape[1])).T
    hidden = w_out_ref.shape[1]
    w_wide_ref[...] = jnp.concatenate(
        [w_out_ref[...].astype(F32), jnp.zeros((2 * GROUP - channels, hidden), F32)], axis=0
    ).T.astype(BF16)


def dot(a, b):
    return jnp.dot(a, b, preferred_element_type=F32)


def dot_nt(a, b):
    return lax.dot_general(a, b, (((1,), (1,)), ((), ())), preferred_element_type=F32)


def sigmoid(v):
    return 0.5 * jnp.tanh(0.5 * v) + 0.5


def closure_kernel(
    entries,
    squares_ref, xs_ref, og_ref, w_in_ref, b_in_ref, w_mid_ref, w_mid_t_ref, b_col_ref, w_out_ref,
    back_ref, sums_ref,
    mid_ref, in_ref, out_ref,
):
    cells = xs_ref.shape[0]
    channels, hidden = w_in_ref.shape
    total = jnp.sum(squares_ref[...], axis=0, keepdims=True)
    inv_norm = lax.rsqrt(total / entries + EPS)[:, :1]
    weights = jnp.concatenate(
        [inv_norm * w_in_ref[...], b_in_ref[...], jnp.zeros((GROUP - channels - 1, hidden), F32)], axis=0
    )
    high = weights.astype(BF16).astype(F32)
    low = weights - high
    pair = jnp.concatenate([high, low], axis=0).astype(BF16)
    first = jnp.concatenate([high, high, low, jnp.zeros_like(low)], axis=0).T.astype(BF16)
    mid_ref[...] = jnp.zeros_like(mid_ref)
    in_ref[...] = jnp.zeros_like(in_ref)
    out_ref[...] = jnp.zeros_like(out_ref)

    def step(t, carry):
        x = xs_ref[t]
        og = og_ref[t]
        pre_first = dot(first, x)
        gate = sigmoid(pre_first)
        act = pre_first * gate
        slope_one = gate + act * (1.0 - gate)
        hidden_one = act.astype(BF16)
        pre_second = dot(w_mid_t_ref[...], hidden_one) + b_col_ref[:, :1]
        gate = sigmoid(pre_second)
        act = pre_second * gate
        slope_two = gate + act * (1.0 - gate)
        hidden_two = act.astype(BF16)
        delta_two = (dot(w_out_ref[...], og) * slope_two).astype(BF16)
        delta_one = (dot(w_mid_ref[...], delta_two) * slope_one).astype(BF16)
        mid_ref[...] += dot_nt(jnp.concatenate([hidden_one, og], axis=0), delta_two)
        out_ref[...] += dot_nt(og, hidden_two)
        in_ref[...] += dot_nt(x[: 2 * GROUP], delta_one)
        back = dot(pair, delta_one)
        back = back[:GROUP] + back[GROUP:]
        place = pl.ds(pl.multiple_of(t * GROUP, GROUP), GROUP)
        for q in range(back_ref.shape[0]):
            back_ref[q, place, :] = back[:, q * LANES : (q + 1) * LANES]
        return carry

    lax.fori_loop(0, cells, step, 0)
    c = channels
    sums = in_ref[...]
    extra = jnp.concatenate(
        [
            (sums[:c] + sums[GROUP : GROUP + c]) * inv_norm,
            sums[c : c + 1],
            jnp.zeros((GROUP - c - 1, hidden), F32),
            out_ref[:c],
            mid_ref[hidden + c : hidden + c + 1],
            jnp.zeros((GROUP - c - 1, hidden), F32),
        ],
        axis=0,
    )
    sums_ref[:hidden, :] = mid_ref[:hidden, :LANES]
    sums_ref[hidden : 2 * hidden, :] = mid_ref[:hidden, LANES:]
    sums_ref[2 * hidden : 2 * hidden + 2 * GROUP, :] = extra[:, :LANES]
    sums_ref[2 * hidden + 2 * GROUP :, :] = extra[:, LANES:]


def finish_kernel(
    tags_ref, adj_ref, back_ref, left_ref, right_ref, front_ref, rear_ref, out_ref
):
    channels, cells, line = adj_ref.shape
    span = cells // 2
    lane = lax.broadcasted_iota(jnp.int32, (cells, line), 1)
    row = lax.broadcasted_iota(jnp.int32, (cells, line), 0)
    node = lax.rem(lane, NODES)
    a, b, c3 = node // 16, lax.rem(node // 4, 4), lax.rem(node, 4)
    bottom = jnp.zeros((cells, line), F32)
    top = jnp.zeros((cells, line), F32)
    for r in range(cells):
        bottom = jnp.where(row == r, 1.0 - 2.0 * tags_ref[0, r // span, r % span].astype(F32), bottom)
        top = jnp.where(row == r, 1.0 - 2.0 * tags_ref[1, r // span, r % span].astype(F32), top)
    low_wall = lane < NODES
    high_wall = lane >= line - NODES
    for c in range(channels):
        v = adj_ref[c]
        lx = jnp.concatenate([left_ref[c], v[:span]], axis=0)
        ux = jnp.concatenate([v[span:], right_ref[c]], axis=0)
        lz = jnp.concatenate([front_ref[c, 0:1], v[: span - 1], front_ref[c, 1:2], v[span : cells - 1]], axis=0)
        uz = jnp.concatenate([v[1:span], rear_ref[c, 0:1], v[span + 1 :], rear_ref[c, 1:2]], axis=0)
        ly = jnp.where(low_wall, bottom * v, pltpu.roll(v, 52, 1))
        uy = jnp.where(high_wall, top * v, pltpu.roll(v, line - 52, 1))
        jump = jnp.where(a == 0, pltpu.roll(lx, line - 48, 1) - v, 0.0)
        jump += jnp.where(a == 3, pltpu.roll(ux, 48, 1) - v, 0.0)
        jump += jnp.where(b == 0, ly - v, 0.0)
        jump += jnp.where(b == 3, uy - v, 0.0)
        jump += jnp.where(c3 == 0, pltpu.roll(lz, line - 3, 1) - v, 0.0)
        jump += jnp.where(c3 == 3, pltpu.roll(uz, 3, 1) - v, 0.0)
        back = jnp.concatenate(
            [back_ref[q, pl.ds(c, cells, stride=GROUP), :] for q in range(line // LANES)], axis=1
        )
        total = v + (0.5 * KAPPA) * jump + back
        out_ref[c, 0] = total[:span]
        out_ref[c, 1] = total[span:]


def unpack_kernel(sums_ref, in_ref, b_in_ref, mid_ref, b_mid_ref, out_ref):
    channels, hidden = in_ref.shape
    mid_ref[:, :LANES] = sums_ref[:hidden, :]
    mid_ref[:, LANES:] = sums_ref[hidden : 2 * hidden, :]
    extra = jnp.concatenate(
        [sums_ref[2 * hidden : 2 * hidden + 2 * GROUP, :], sums_ref[2 * hidden + 2 * GROUP :, :]], axis=1
    )
    in_ref[...] = extra[:channels]
    b_in_ref[...] = extra[channels : channels + 1]
    out_ref[...] = extra[GROUP : GROUP + channels]
    b_mid_ref[...] = extra[GROUP + channels : GROUP + channels + 1]


def shape(*dims, dtype=F32):
    return jax.ShapeDtypeStruct(dims, dtype)


def run_squares(state, peers):
    return pl.pallas_call(
        squares_kernel,
        out_shape=shape(peers, LANES),
        in_specs=whole_vmem(1),
        out_specs=whole_vmem(1)[0],
        name="squares",
    )(state)


def run_unpack(sums, channels):
    hidden = (sums.shape[0] - 4 * GROUP) // 2
    return pl.pallas_call(
        unpack_kernel,
        out_shape=(
            shape(channels, hidden),
            shape(1, hidden),
            shape(hidden, hidden),
            shape(1, hidden),
            shape(channels, hidden),
        ),
        in_specs=whole_vmem(1),
        out_specs=tuple(whole_vmem(5)),
        name="unpack",
    )(sums)


def run_adjoint(state, cotangent, local_inverse, w_mid, b_mid, w_out):
    channels, _, span, line = state.shape
    cells = 2 * span
    hidden = w_mid.shape[0]
    return pl.pallas_call(
        adjoint_kernel,
        out_shape=(
            shape(channels, cells, line),
            shape(cells, 2 * GROUP, line, dtype=BF16),
            shape(cells, 4 * GROUP, line, dtype=BF16),
            shape(hidden, hidden, dtype=BF16),
            shape(hidden, LANES),
            shape(hidden, 2 * GROUP, dtype=BF16),
            shape(channels, span, line),
            shape(channels, span, line),
            shape(channels, 2, line),
            shape(channels, 2, line),
        ),
        in_specs=whole_vmem(6),
        out_specs=tuple(whole_vmem(10)),
        scratch_shapes=[pltpu.VMEM((line // LANES, cells * GROUP, LANES), F32)],
        name="adjoint",
    )(state, cotangent, local_inverse, w_mid, b_mid.reshape(1, hidden), w_out.T)


def run_closure(entries, squares, xs, og, w_in, b_in, w_mid, w_mid_t, b_col, w_out):
    cells, _, line = xs.shape
    _, hidden = w_in.shape
    return pl.pallas_call(
        functools.partial(closure_kernel, entries),
        out_shape=(
            shape(line // LANES, cells * GROUP, LANES),
            shape(2 * hidden + 4 * GROUP, LANES),
        ),
        in_specs=whole_vmem(9),
        out_specs=tuple(whole_vmem(2)),
        scratch_shapes=[
            pltpu.VMEM((hidden + 2 * GROUP, hidden), F32),
            pltpu.VMEM((2 * GROUP, hidden), F32),
            pltpu.VMEM((2 * GROUP, hidden), F32),
        ],
        name="closure",
    )(squares, xs, og, w_in, b_in.reshape(1, hidden), w_mid, w_mid_t, b_col, w_out)


def run_finish(tags, adjoint, back, left, right, front, rear):
    channels, cells, line = adjoint.shape
    return pl.pallas_call(
        finish_kernel,
        out_shape=shape(channels, 2, cells // 2, line),
        in_specs=[pl.BlockSpec(memory_space=pltpu.SMEM)] + whole_vmem(6),
        out_specs=pl.BlockSpec(memory_space=pltpu.VMEM),
        name="finish",
    )(tags, adjoint, back, left, right, front, rear)


def ring(count, step):
    return [(i, (i + step) % count) for i in range(count)]


def exchange(value, axes):
    return lax.all_to_all(value, axes, 0, 0, tiled=True)


def per_device(state, cotangent, local_inverse, wall_tags, w_in, b_in, w_mid, b_mid, w_out):
    channels, x_elems, z_elems, line = state.shape
    gx, gz = lax.axis_size(GX), lax.axis_size(GZ)
    devices = gx * gz
    nodes = x_elems * z_elems * line * devices
    plane, tower = lax.axis_size(PLANE), lax.axis_size(TOWER)
    squares = run_squares(state, devices).reshape(devices, 1, LANES)
    squares = exchange(squares, AXES)
    adjoint, og, xs, w_mid_t, b_col, w_wide, low_x, high_x, low_z, high_z = run_adjoint(
        state, cotangent, local_inverse, w_mid, b_mid, w_out
    )
    sends = ((high_x, GX, gx, 1), (low_x, GX, gx, -1), (high_z, GZ, gz, 1), (low_z, GZ, gz, -1))
    halo = []
    for face, axes, count, way in sends:
        halo.append(lax.ppermute(face, axes, ring(count, way)))
    back, sums = run_closure(
        float(channels * nodes), squares.reshape(devices, LANES), xs, og, w_in, b_in, w_mid,
        w_mid_t, b_col, w_wide,
    )
    grad_state = run_finish(wall_tags, adjoint, back, *halo)
    factor = 4.0 / math.sqrt(nodes)
    width = sums.shape[0] // plane
    part = exchange(sums.reshape(plane, width, 1, LANES), PLANE)
    part = jnp.broadcast_to(jnp.sum(part, axis=0, keepdims=True), (tower, width, 1, LANES))
    part = exchange(part, TOWER)
    part = factor * jnp.sum(part, axis=0, keepdims=True)
    part = jnp.broadcast_to(part, (plane, width, 1, LANES))
    part = exchange(part, PLANE)
    grad_in, grad_b_in, grad_mid, grad_b_mid, grad_out = run_unpack(part.reshape(sums.shape), channels)
    return grad_state, grad_in, grad_b_in[0], grad_mid, grad_b_mid[0], grad_out.T


def solution(mesh):
    fine = Mesh(mesh.devices.reshape(2, 4, 4, 4, 2), AXES)
    block = P(None, GX, GZ, None)
    placed = (block, block, block, P(None, GX, GZ)) + (P(),) * 5
    return jax.shard_map(
        per_device,
        mesh=fine,
        in_specs=placed,
        out_specs=(block, P(), P(), P(), P(), P()),
        check_vma=False,
    )
```
